32 devices in a mesh: bas: 8 (over y, x, core), aux: 4 (over z).
Axes of the slice: x: 2, y: 2, z: 4, core: 2. Of those that a mesh axis runs over, the one named last changes fastest.
Arguments:
- integrals: bfloat16 [4, 8192, 8192], P('aux', 'bas'), may hold values from -6 to 6
- screen: int32 [4, 64, 64], P('aux', 'bas'), may hold values from 0 to 1, as said below
- coefficients: bfloat16 [8192, 384], P('bas'), may hold values from -0.0625 to 0.0625
- weights: float32 [384], replicated, may hold values from -2 to 2
Outputs:
- exchange: bfloat16 [8192, 8192], P('aux', 'bas')
The draws below stay inside these ranges and needn't reach their ends.
Inputs may be any that keep to these rules, and one draw needn't show every extreme that they name: `screen`: every block with equal row and column block index is 1; the share of ones differs from row block to row block.
All inputs are finite; a program needn't handle non-finite values.
Results may differ from the reference program's by a relative error of at most 0.018.
Values may be sent and summed in bfloat16 or wider, within the bound.
A program may use at most 128 MiB of HBM per device.

```python
import math
import jax
import jax.numpy as jnp
from jax import lax

NBF = 8192
NOCC = 384
BLOCK = 128
AUX_DEV = 1
NAUX = 4
NB = 64
N_AUX = 4


def draw_screen(key, part):
    first_key, second_key = jax.random.split(jax.random.fold_in(key, 17))
    levels = jax.random.randint(first_key, (1, NB, 1), 15, 96)
    values = jax.random.randint(second_key, (NAUX, NB, NB), 0, 100)
    kept = (values < levels).astype(jnp.int32)
    diagonal = jnp.eye(NB, dtype=jnp.int32)[None, :, :]
    return jnp.maximum(kept, diagonal)


def block_scale(own_key, extent, cuts, least, top_value):
    def one(position, blocks):
        heights = jax.random.uniform(jax.random.fold_in(jax.random.fold_in(own_key, 6), position), (blocks,), jnp.float32, least / len(cuts), top_value / len(cuts))
        return jnp.repeat(jnp.exp(heights), extent[position] // blocks).reshape((-1,) + (1,) * (len(extent) - position - 1))

    level = one(*cuts[0])
    for cut in cuts[1:]:
        level = level * one(*cut)
    return level


def centred(stream_key, shape, width, reach, pieces=(), kind=jnp.bfloat16):
    values = jax.random.normal(stream_key, shape, jnp.float32) * width
    if len(pieces) > 0:
        values = block_scale(stream_key, shape, pieces, -0.22, 0.18) * values
    return jnp.clip(values, min=-reach, max=reach).astype(kind)


def setup_inputs(seed: int = 0) -> dict:
    splits = jax.random.split(jax.random.key(seed), 5)
    integrals = centred(splits[0], (NAUX, NBF, NBF), 1.0, 6.0, ((0, 4), (1, 8)))
    screen = draw_screen(jax.random.fold_in(splits[4], 71), 0)
    coefficients = centred(splits[2], (NBF, NOCC), NBF ** -0.5, 0.0625, ((0, 8),))
    weights = jnp.clip(jax.random.uniform(splits[3], (NOCC,), jnp.float32, -2.0, 2.0), -2.0, 2.0)
    return {"integrals": integrals, "screen": screen, "coefficients": coefficients, "weights": weights}


def reference(integrals, screen, coefficients, weights):
    nblk = NBF // BLOCK
    blocks = integrals.reshape(N_AUX, AUX_DEV, nblk, BLOCK, nblk, BLOCK)
    masks = screen.reshape(N_AUX, AUX_DEV, nblk, 1, nblk, 1).astype(jnp.bfloat16)
    tiled = jnp.tile(weights, AUX_DEV)
    factor = coefficients.astype(jnp.float32)

    def accumulate(total, pair):
        block, mask = pair
        masked = (block * mask).reshape(AUX_DEV, NBF, NBF)
        half = jnp.einsum('pml,li->mpi', masked.astype(jnp.float32), factor)
        half = half.reshape(NBF, AUX_DEV * NOCC).astype(jnp.bfloat16)
        weighted = (half.astype(jnp.float32) * tiled).astype(jnp.bfloat16)
        term = lax.dot_general(half, weighted, (((1,), (1,)), ((), ())), preferred_element_type=jnp.float32)
        rounded = lax.optimization_barrier(term.astype(jnp.bfloat16))
        return (total + rounded.astype(jnp.float32), None)
    start_total = jnp.zeros((NBF, NBF), jnp.float32)
    total, _ = lax.scan(accumulate, start_total, (blocks, masks))
    return (total * (1.0 / math.sqrt(NAUX * NOCC))).astype(jnp.bfloat16)
```

```python
import functools
import math

import jax
import jax.numpy as jnp
from jax import lax
from jax.experimental import pallas as pl
from jax.experimental.pallas import tpu as pltpu
from jax.sharding import PartitionSpec as P

BLOCK = 128
LANES = 128


def kernel(groups, aux, scale, integrals, screen, coefs, weights, out,
           ints, fac, acc, right, left, wt, total, result,
           load_sem, ring_send, ring_recv, pair_send, pair_recv,
           line_recv, up_send, down_send,
           lring_send, lring_recv, lpair_send, lpair_recv, lown_sem, out_sem):
    rows, basis = ints.shape
    chunks = fac.shape[0]
    half_rows = rows // 2
    spread = left.shape[1]
    sets = spread // 2
    row_blocks = rows // BLOCK
    col_blocks = basis // BLOCK
    bas_me = lax.axis_index("bas")
    z = lax.axis_index("aux")
    core = bas_me % 2
    half_ring = groups // 2

    def swap(index):
        upper = index // half_ring
        return index + upper * (3 * half_ring - 1 - 2 * index)

    pos = swap(bas_me // 2)

    def device_at(position, which):
        return 2 * swap(position % groups) + which

    partner = bas_me - core + (1 - core)

    def ring_to(half):
        return device_at(pos + groups + 1 - 2 * half, core)

    def remote(src, dst, send, recv, bas=None, aux_to=None):
        return pltpu.make_async_remote_copy(
            src_ref=src, dst_ref=dst, send_sem=send, recv_sem=recv,
            device_id={"bas": bas_me if bas is None else bas, "aux": z if aux_to is None else aux_to},
            device_id_type=pl.DeviceIdType.MESH)

    finish = []

    load_groups = 8
    load_cols = basis // load_groups

    def int_load(i):
        cols = pl.ds(i * load_cols, load_cols)
        return pltpu.make_async_copy(integrals.at[0, :, cols], ints.at[:, cols], load_sem.at[chunks + i])

    def fac_load(j):
        return pltpu.make_async_copy(coefs.at[:, pl.ds(j * LANES, LANES)], fac.at[j, bas_me], load_sem.at[j])

    for j in range(chunks):
        fac_load(j).start()
    for i in range(load_groups):
        int_load(i).start()

    barrier = pltpu.get_barrier_semaphore()
    for other in (ring_to(0), ring_to(1), partner):
        pl.semaphore_signal(barrier, inc=1, device_id={"bas": other, "aux": z}, device_id_type=pl.DeviceIdType.MESH)

    @pl.when(z > 0)
    def _():
        pl.semaphore_signal(barrier, inc=1, device_id={"bas": bas_me, "aux": z - 1}, device_id_type=pl.DeviceIdType.MESH)

    @pl.when(z < aux - 1)
    def _():
        pl.semaphore_signal(barrier, inc=1, device_id={"bas": bas_me, "aux": z + 1}, device_id_type=pl.DeviceIdType.MESH)

    peers = 3 + (z + aux - 1) // aux + (2 * aux - 2 - z) // aux
    pl.semaphore_wait(barrier, peers)

    def origin(h, half, which):
        return device_at(pos + groups - h + 2 * h * half, which)

    def fac_piece(j, h, half, which):
        return fac.at[j, origin(h, half, which), pl.ds(half * half_rows, half_rows)]

    def ring_copy(j, h, half):
        piece = fac_piece(j, h, half, core)
        return remote(piece, piece, ring_send.at[j, h, half], ring_recv.at[j, h, half], bas=ring_to(half))

    def pair_copy(j, h, half):
        piece = fac_piece(j, h, half, core)
        return remote(piece, piece, pair_send.at[j, h, half], pair_recv.at[j, h, half], bas=partner)

    def pass_on(j, h, half):
        if h < groups - 1:
            ring_copy(j, h, half).start()
            finish.append(ring_copy(j, h, half).wait_send)
        pair_copy(j, h, half).start()
        finish.append(pair_copy(j, h, half).wait_send)

    def ring_own(j):
        fac_load(j).wait()
        for half in (0, 1):
            pass_on(j, 0, half)

    def ring_step(j, h):
        for half in (0, 1):
            piece = fac_piece(j, h, half, core)
            remote(piece, piece, ring_send.at[j, h - 1, half], ring_recv.at[j, h - 1, half], bas=ring_to(half)).wait_recv()
            pass_on(j, h, half)

    def pair_wait(j, h):
        for half in (0, 1):
            piece = fac_piece(j, h, half, 1 - core)
            remote(piece, piece, pair_send.at[j, h, half], pair_recv.at[j, h, half], bas=partner).wait_recv()

    def mask_group(i):
        int_load(i).wait()
        per = col_blocks // load_groups

        def body(q, carry):
            column = i * per + q
            cols = pl.ds(pl.multiple_of(column * BLOCK, BLOCK), BLOCK)
            for r in range(row_blocks):
                keep = screen[0, r, column].astype(jnp.float32)
                keep = jnp.full((BLOCK, BLOCK), keep, jnp.float32).astype(jnp.bfloat16)
                ints[pl.ds(r * BLOCK, BLOCK), cols] = ints[pl.ds(r * BLOCK, BLOCK), cols] * keep
            return carry

        lax.fori_loop(0, per, body, 0)

    tile_m = min(256, rows)
    fine = half_rows % LANES == 0

    def piece_dot(j, block, start, length, first):
        def body(m, carry):
            at = pl.ds(pl.multiple_of(m * tile_m, tile_m), tile_m)
            cols = pl.ds(pl.multiple_of(block * rows + start, LANES), length)
            part = jnp.dot(ints[at, cols], fac[j, block, pl.ds(start, length), :],
                           preferred_element_type=jnp.float32)
            acc[at, :] = part if first else acc[at, :] + part
            return carry

        lax.fori_loop(0, rows // tile_m, body, 0)

    def half_dots(j, h):
        pair_wait(j, h)
        if fine:
            if h == 0:
                piece_dot(j, bas_me, 0, rows, True)
                piece_dot(j, partner, 0, rows, False)
            else:
                for half in (0, 1):
                    for which in (core, 1 - core):
                        piece_dot(j, origin(h, half, which), half * half_rows, half_rows, False)
        elif h == groups - 1:
            acc[...] = jnp.zeros_like(acc)

            def body(block, carry):
                piece_dot(j, block, 0, rows, False)
                return carry

            lax.fori_loop(0, 2 * groups, body, 0)

    def weigh(j, p):
        values = right[j, p].astype(jnp.float32) * weights[:, pl.ds(j * LANES, LANES)]
        wt[j, pl.ds(pl.multiple_of(p * LANES, LANES), LANES), :] = values.T.astype(jnp.bfloat16)

    def up_copy(j, p):
        return remote(right.at[j, p], right.at[j, p], up_send.at[j, p], line_recv.at[j, p], aux_to=z + 1)

    def down_copy(j, p):
        return remote(right.at[j, p], right.at[j, p], down_send.at[j, p], line_recv.at[j, p], aux_to=z - 1)

    def guard(condition, action):
        pl.when(condition)(lambda: action())

    def send_up(j, p, condition):
        condition = condition & (z < aux - 1)
        guard(condition, lambda: up_copy(j, p).start())
        finish.append(lambda: guard(condition, lambda: up_copy(j, p).wait_send()))

    def send_down(j, p, condition):
        condition = condition & (z > 0)
        guard(condition, lambda: down_copy(j, p).start())
        finish.append(lambda: guard(condition, lambda: down_copy(j, p).wait_send()))

    def left_piece(ref_index, half):
        j, s, p = ref_index
        return left.at[j, s, p, pl.ds(half * half_rows, half_rows)]

    def lring_copy(src, j, t, p, half):
        return remote(src, left_piece((j, 2 * t + core, p), half),
                      lring_send.at[j, t, p, half], lring_recv.at[j, t, p, half], bas=ring_to(half))

    def lpair_copy(src, j, t, p, half):
        return remote(src, left_piece((j, 2 * t + core, p), half),
                      lpair_send.at[j, t, p, half], lpair_recv.at[j, t, p, half], bas=partner)

    def lown_copy(j, t, p):
        return pltpu.make_async_copy(right.at[j, p], left.at[j, 2 * t + core, p], lown_sem.at[j, t, p])

    def away(t):
        return (pos - swap(z * sets + t) + groups) % groups

    def left_start(j, p, condition):
        for t in range(sets):
            mine = condition & (away(t) == 0)

            def go(t=t):
                for half in (0, 1):
                    src = right.at[j, p, pl.ds(half * half_rows, half_rows)]
                    lring_copy(src, j, t, p, half).start()
                    lpair_copy(src, j, t, p, half).start()
                lown_copy(j, t, p).start()

            def end(t=t):
                for half in (0, 1):
                    src = right.at[j, p, pl.ds(half * half_rows, half_rows)]
                    lring_copy(src, j, t, p, half).wait_send()
                    lpair_copy(src, j, t, p, half).wait_send()

            guard(mine, go)
            finish.append(lambda mine=mine, end=end: guard(mine, end))

    def left_step(j, p, condition):
        for t in range(sets):
            distance = away(t)
            near = (2 * distance) // (groups + 1)
            other = condition & (distance != 0)
            mine = condition & (distance == 0)
            for half in (near, 1 - near):
                hops = distance + half * (groups - 2 * distance)
                src = left_piece((j, 2 * t + core, p), half)

                def go(t=t, half=half, src=src):
                    lring_copy(src, j, t, p, half).wait_recv()
                    lpair_copy(src, j, t, p, half).start()

                def onward(t=t, half=half, src=src):
                    lring_copy(src, j, t, p, half).start()

                def end(t=t, half=half, src=src):
                    lpair_copy(src, j, t, p, half).wait_send()

                def end_onward(t=t, half=half, src=src):
                    lring_copy(src, j, t, p, half).wait_send()

                further = other & (hops < groups - 1)
                guard(other, go)
                guard(further, onward)
                finish.append(lambda other=other, end=end: guard(other, end))
                finish.append(lambda further=further, end=end_onward: guard(further, end))

            def own(t=t):
                lown_copy(j, t, p).wait()

            guard(mine, own)

            def from_partner(t=t):
                for half in (0, 1):
                    dst = left_piece((j, 2 * t + 1 - core, p), half)
                    remote(dst, dst, lpair_send.at[j, t, p, half], lpair_recv.at[j, t, p, half], bas=partner).wait_recv()

            guard(condition, from_partner)

    always = z >= 0

    def members(d):
        if d == 0:
            return [(z, always)]
        return [(z - d, z - d >= 0), (z + d, z + d < aux)]

    def line_event(j, d):
        for p, there in members(d):
            if d == 0:
                send_up(j, p, there)
                send_down(j, p, there)
            elif p is not None:
                guard(there, lambda p=p: up_copy(j, p).wait_recv())
        if d > 0:
            below, above = members(d)
            send_up(j, below[0], below[1])
            send_down(j, above[0], above[1])
        for p, there in members(d):
            left_start(j, p, there)
        if d > 0:
            for p, there in members(d):
                guard(there, lambda p=p: weigh(j, p))

    def left_event(j, d):
        for p, there in members(d):
            left_step(j, p, there)

    def close_half(j):
        right[j, z] = acc[...].astype(jnp.bfloat16)
        weigh(j, z)
        line_event(j, 0)

    tile_n = min(256, rows)
    tiles_in = rows // tile_n
    tiles = spread * tiles_in

    def out_copy(i):
        at = pl.ds(i * tile_n, tile_n)
        return pltpu.make_async_copy(result.at[at], out.at[at], out_sem.at[i])

    def exchange(j, low, high):
        def body(i, carry):
            s, r = i // tiles_in, i % tiles_in
            at = pl.ds(pl.multiple_of(r * tile_n, tile_n), tile_n)
            lhs = jnp.concatenate([left[j, s, p, at, :] for p in range(aux)], axis=1)
            part = jnp.dot(lhs, wt[j], preferred_element_type=jnp.float32)
            to = pl.ds(pl.multiple_of(i * tile_n, tile_n), tile_n)
            if j > 0:
                part = total[to, :] + part
            if j == chunks - 1:
                result[to, :] = (part * scale).astype(jnp.bfloat16)
            else:
                total[to, :] = part
            return carry

        lax.fori_loop(low, high, body, 0)

    ring_own(0)
    if chunks > 1:
        ring_own(1)
    for i in range(load_groups // 2):
        mask_group(i)
    ring_step(0, 1)
    for i in range(load_groups // 2, load_groups):
        mask_group(i)
    for h in range(1, groups):
        if h > 1:
            ring_step(0, h)
        if h == groups - 1 and chunks > 2:
            ring_own(2)
        if chunks > 1:
            ring_step(1, h)
        half_dots(0, h - 1)
    half_dots(0, groups - 1)
    close_half(0)
    events = []
    for j in range(chunks):
        for d in range(1, aux):
            events.append((j, d))
    for j in range(1, chunks):
        for h in range(groups):
            half_dots(j, h)
            if j + 1 < chunks and h + 1 < groups:
                ring_step(j + 1, h + 1)
        close_half(j)
        if j + 2 < chunks:
            ring_own(j + 2)
    behind = [(j, d) for j in range(chunks) for d in range(aux)]
    work = []
    for n, (j, d) in enumerate(events):
        line_event(j, d)
        while behind and behind[0] < (j, d):
            entry = behind.pop(0)
            left_event(*entry)
            if entry[1] == aux - 1:
                step = -(-tiles // max(1, aux - 1))
                work += [(entry[0], low, min(tiles, low + step)) for low in range(0, tiles, step)]
        if work:
            exchange(*work.pop(0))
    while behind:
        left_event(*behind.pop(0))
    for item in work:
        exchange(*item)
    parts = 4 if tiles % 4 == 0 else 1
    for i in range(parts):
        low, high = i * tiles // parts, (i + 1) * tiles // parts
        exchange(chunks - 1, low, high)
        if i > 0:
            for n in range((i - 1) * tiles // parts, low):
                out_copy(n).start()
    for n in range((parts - 1) * tiles // parts, tiles):
        out_copy(n).start()
    for action in finish:
        action()
    for n in range(tiles):
        out_copy(n).wait()


def shards(integrals, screen, coefficients, weights):
    _, rows, basis = integrals.shape
    occ = coefficients.shape[1]
    bas, aux = lax.axis_size("bas"), lax.axis_size("aux")
    groups, spread, chunks = bas // 2, bas // aux, occ // LANES
    sets = spread // 2
    tiles = spread * rows // min(256, rows)
    scale = 1.0 / math.sqrt(integrals.shape[0] * aux * occ)
    dma = pltpu.SemaphoreType.DMA
    bf16, f32 = jnp.bfloat16, jnp.float32
    return pl.pallas_call(
        functools.partial(kernel, groups, aux, scale),
        out_shape=jax.ShapeDtypeStruct((spread * rows, rows), bf16),
        in_specs=[
            pl.BlockSpec(memory_space=pl.ANY),
            pl.BlockSpec(memory_space=pltpu.SMEM),
            pl.BlockSpec(memory_space=pl.ANY),
            pl.BlockSpec(memory_space=pltpu.VMEM),
        ],
        out_specs=pl.BlockSpec(memory_space=pl.ANY),
        scratch_shapes=[
            pltpu.VMEM((rows, basis), bf16),
            pltpu.VMEM((chunks, bas, rows, LANES), bf16),
            pltpu.VMEM((rows, LANES), f32),
            pltpu.VMEM((chunks, aux, rows, LANES), bf16),
            pltpu.VMEM((chunks, spread, aux, rows, LANES), bf16),
            pltpu.VMEM((chunks, aux * LANES, rows), bf16),
            pltpu.VMEM((spread * rows, rows), f32),
            pltpu.VMEM((spread * rows, rows), bf16),
            dma((chunks + 8,)),
            dma((chunks, groups, 2)), dma((chunks, groups, 2)),
            dma((chunks, groups, 2)), dma((chunks, groups, 2)),
            dma((chunks, aux)), dma((chunks, aux)), dma((chunks, aux)),
            dma((chunks, sets, aux, 2)), dma((chunks, sets, aux, 2)),
            dma((chunks, sets, aux, 2)), dma((chunks, sets, aux, 2)),
            dma((chunks, sets, aux)),
            dma((tiles,)),
        ],
        compiler_params=pltpu.CompilerParams(
            collective_id=0, has_side_effects=True, vmem_limit_bytes=62 * 1024 * 1024),
    )(integrals, screen, coefficients, weights.reshape(1, occ))


def solution(mesh):
    in_specs = (P("aux", "bas", None), P("aux", "bas", None), P("bas", None), P())
    out_specs = P("aux", "bas")
    return jax.shard_map(shards, mesh=mesh, in_specs=in_specs, out_specs=out_specs, check_vma=False)
```

```python
import functools
import math

import jax
import jax.numpy as jnp
from jax import lax
from jax.experimental import pallas as pl
from jax.experimental.pallas import tpu as pltpu
from jax.sharding import PartitionSpec as P

BLOCK = 128
LANES = 128


def kernel(groups, aux, scale, integrals, screen, coefs, weights, out,
           ints, fac, acc, right, left, wt, total, result,
           load_sem, ring_send, ring_recv, pair_send, pair_recv,
           line_recv, up_send, down_send,
           lring_send, lring_recv, lpair_send, lpair_recv, lown_sem, out_sem):
    rows, basis = ints.shape
    chunks = fac.shape[0]
    half_rows = rows // 2
    spread = left.shape[1]
    sets = spread // 2
    row_blocks = rows // BLOCK
    col_blocks = basis // BLOCK
    bas_me = lax.axis_index("bas")
    z = lax.axis_index("aux")
    core = bas_me % 2
    half_ring = groups // 2

    def swap(index):
        upper = index // half_ring
        return index + upper * (3 * half_ring - 1 - 2 * index)

    pos = swap(bas_me // 2)

    def device_at(position, which):
        return 2 * swap(position % groups) + which

    partner = bas_me - core + (1 - core)

    def ring_to(half):
        return device_at(pos + groups + 1 - 2 * half, core)

    def remote(src, dst, send, recv, bas=None, aux_to=None):
        return pltpu.make_async_remote_copy(
            src_ref=src, dst_ref=dst, send_sem=send, recv_sem=recv,
            device_id={"bas": bas_me if bas is None else bas, "aux": z if aux_to is None else aux_to},
            device_id_type=pl.DeviceIdType.MESH)

    finish = []

    load_groups = 8
    load_cols = basis // load_groups

    def int_load(i):
        cols = pl.ds(i * load_cols, load_cols)
        return pltpu.make_async_copy(integrals.at[0, :, cols], ints.at[:, cols], load_sem.at[chunks + i])

    def fac_load(j):
        return pltpu.make_async_copy(coefs.at[:, pl.ds(j * LANES, LANES)], fac.at[j, bas_me], load_sem.at[j])

    for j in range(chunks):
        fac_load(j).start()
    for i in range(load_groups):
        int_load(i).start()

    barrier = pltpu.get_barrier_semaphore()
    for other in (ring_to(0), ring_to(1), partner):
        pl.semaphore_signal(barrier, inc=1, device_id={"bas": other, "aux": z}, device_id_type=pl.DeviceIdType.MESH)

    @pl.when(z > 0)
    def _():
        pl.semaphore_signal(barrier, inc=1, device_id={"bas": bas_me, "aux": z - 1}, device_id_type=pl.DeviceIdType.MESH)

    @pl.when(z < aux - 1)
    def _():
        pl.semaphore_signal(barrier, inc=1, device_id={"bas": bas_me, "aux": z + 1}, device_id_type=pl.DeviceIdType.MESH)

    peers = 3 + (z + aux - 1) // aux + (2 * aux - 2 - z) // aux
    pl.semaphore_wait(barrier, peers)

    def origin(h, half, which):
        return device_at(pos + groups - h + 2 * h * half, which)

    def fac_piece(j, h, half, which):
        return fac.at[j, origin(h, half, which), pl.ds(half * half_rows, half_rows)]

    def ring_copy(j, h, half):
        piece = fac_piece(j, h, half, core)
        return remote(piece, piece, ring_send.at[j, h, half], ring_recv.at[j, h, half], bas=ring_to(half))

    def pair_copy(j, h, half):
        piece = fac_piece(j, h, half, core)
        return remote(piece, piece, pair_send.at[j, h, half], pair_recv.at[j, h, half], bas=partner)

    def pass_on(j, h, half):
        if h < groups - 1:
            ring_copy(j, h, half).start()
            finish.append(ring_copy(j, h, half).wait_send)
        pair_copy(j, h, half).start()
        finish.append(pair_copy(j, h, half).wait_send)

    def ring_own(j):
        fac_load(j).wait()
        for half in (0, 1):
            pass_on(j, 0, half)

    def ring_step(j, h):
        for half in (0, 1):
            piece = fac_piece(j, h, half, core)
            remote(piece, piece, ring_send.at[j, h - 1, half], ring_recv.at[j, h - 1, half], bas=ring_to(half)).wait_recv()
            pass_on(j, h, half)

    def pair_wait(j, h):
        for half in (0, 1):
            piece = fac_piece(j, h, half, 1 - core)
            remote(piece, piece, pair_send.at[j, h, half], pair_recv.at[j, h, half], bas=partner).wait_recv()

    def mask_group(i):
        int_load(i).wait()
        per = col_blocks // load_groups

        def body(q, carry):
            column = i * per + q
            cols = pl.ds(pl.multiple_of(column * BLOCK, BLOCK), BLOCK)
            for r in range(row_blocks):
                keep = screen[0, r, column].astype(jnp.float32)
                keep = jnp.full((BLOCK, BLOCK), keep, jnp.float32).astype(jnp.bfloat16)
                ints[pl.ds(r * BLOCK, BLOCK), cols] = ints[pl.ds(r * BLOCK, BLOCK), cols] * keep
            return carry

        lax.fori_loop(0, per, body, 0)

    tile_m = min(256, rows)
    fine = half_rows % LANES == 0

    def piece_dot(j, block, start, length, first):
        def body(m, carry):
            at = pl.ds(pl.multiple_of(m * tile_m, tile_m), tile_m)
            cols = pl.ds(pl.multiple_of(block * rows + start, LANES), length)
            part = jnp.dot(ints[at, cols], fac[j, block, pl.ds(start, length), :],
                           preferred_element_type=jnp.float32)
            acc[j, at, :] = part if first else acc[j, at, :] + part
            return carry

        lax.fori_loop(0, rows // tile_m, body, 0)

    def half_dots(j, h):
        pair_wait(j, h)
        if fine:
            if h == 0:
                piece_dot(j, bas_me, 0, rows, True)
                piece_dot(j, partner, 0, rows, False)
            else:
                for half in (0, 1):
                    for which in (core, 1 - core):
                        piece_dot(j, origin(h, half, which), half * half_rows, half_rows, False)
        elif h == groups - 1:
            acc[j] = jnp.zeros(acc.shape[1:], acc.dtype)

            def body(block, carry):
                piece_dot(j, block, 0, rows, False)
                return carry

            lax.fori_loop(0, 2 * groups, body, 0)

    def weigh(j, p):
        values = right[j, p].astype(jnp.float32) * weights[:, pl.ds(j * LANES, LANES)]
        wt[j, pl.ds(pl.multiple_of(p * LANES, LANES), LANES), :] = values.T.astype(jnp.bfloat16)

    def up_copy(j, p):
        return remote(right.at[j, p], right.at[j, p], up_send.at[j, p], line_recv.at[j, p], aux_to=z + 1)

    def down_copy(j, p):
        return remote(right.at[j, p], right.at[j, p], down_send.at[j, p], line_recv.at[j, p], aux_to=z - 1)

    def guard(condition, action):
        pl.when(condition)(lambda: action())

    def send_up(j, p, condition):
        condition = condition & (z < aux - 1)
        guard(condition, lambda: up_copy(j, p).start())
        finish.append(lambda: guard(condition, lambda: up_copy(j, p).wait_send()))

    def send_down(j, p, condition):
        condition = condition & (z > 0)
        guard(condition, lambda: down_copy(j, p).start())
        finish.append(lambda: guard(condition, lambda: down_copy(j, p).wait_send()))

    def left_piece(ref_index, half):
        j, s, p = ref_index
        return left.at[j, s, p, pl.ds(half * half_rows, half_rows)]

    def lring_copy(src, j, t, p, half):
        return remote(src, left_piece((j, 2 * t + core, p), half),
                      lring_send.at[j, t, p, half], lring_recv.at[j, t, p, half], bas=ring_to(half))

    def lpair_copy(src, j, t, p, half):
        return remote(src, left_piece((j, 2 * t + core, p), half),
                      lpair_send.at[j, t, p, half], lpair_recv.at[j, t, p, half], bas=partner)

    def lown_copy(j, t, p):
        return pltpu.make_async_copy(right.at[j, p], left.at[j, 2 * t + core, p], lown_sem.at[j, t, p])

    def away(t):
        return (pos - swap(z * sets + t) + groups) % groups

    def left_start(j, p, condition):
        for t in range(sets):
            mine = condition & (away(t) == 0)

            def go(t=t):
                for half in (0, 1):
                    src = right.at[j, p, pl.ds(half * half_rows, half_rows)]
                    lring_copy(src, j, t, p, half).start()
                    lpair_copy(src, j, t, p, half).start()
                lown_copy(j, t, p).start()

            def end(t=t):
                for half in (0, 1):
                    src = right.at[j, p, pl.ds(half * half_rows, half_rows)]
                    lring_copy(src, j, t, p, half).wait_send()
                    lpair_copy(src, j, t, p, half).wait_send()

            guard(mine, go)
            finish.append(lambda mine=mine, end=end: guard(mine, end))

    def left_stage(j, p, condition, stage):
        for t in range(sets):
            distance = away(t)
            side = (2 * distance) // (groups + 1)
            middle = distance == half_ring
            other = condition & (distance != 0)
            takes = other & (middle if stage == 1 else distance != half_ring)
            halves = (0, 1) if stage == 1 else (side if stage == 0 else 1 - side,)
            for half in halves:
                hops = distance + half * (groups - 2 * distance)
                src = left_piece((j, 2 * t + core, p), half)

                def go(t=t, half=half, src=src):
                    lring_copy(src, j, t, p, half).wait_recv()
                    lpair_copy(src, j, t, p, half).start()

                def onward(t=t, half=half, src=src):
                    lring_copy(src, j, t, p, half).start()

                def end(t=t, half=half, src=src):
                    lpair_copy(src, j, t, p, half).wait_send()

                def end_onward(t=t, half=half, src=src):
                    lring_copy(src, j, t, p, half).wait_send()

                further = takes & (hops < groups - 1)
                guard(takes, go)
                guard(further, onward)
                finish.append(lambda takes=takes, end=end: guard(takes, end))
                finish.append(lambda further=further, end=end_onward: guard(further, end))

    def left_close(j, p, condition):
        for t in range(sets):
            mine = condition & (away(t) == 0)

            def own(t=t):
                lown_copy(j, t, p).wait()

            guard(mine, own)

            def from_partner(t=t):
                for half in (0, 1):
                    dst = left_piece((j, 2 * t + 1 - core, p), half)
                    remote(dst, dst, lpair_send.at[j, t, p, half], lpair_recv.at[j, t, p, half], bas=partner).wait_recv()

            guard(condition, from_partner)

    always = z >= 0

    def members(d):
        if d == 0:
            return [(z, always)]
        return [(z - d, z - d >= 0), (z + d, z + d < aux)]

    def line_event(j, d):
        for p, there in members(d):
            if d == 0:
                send_up(j, p, there)
                send_down(j, p, there)
            elif p is not None:
                guard(there, lambda p=p: up_copy(j, p).wait_recv())
        if d > 0:
            below, above = members(d)
            send_up(j, below[0], below[1])
            send_down(j, above[0], above[1])
        for p, there in members(d):
            left_start(j, p, there)
        if d > 0:
            for p, there in members(d):
                guard(there, lambda p=p: weigh(j, p))

    def close_half(j):
        right[j, z] = acc[j].astype(jnp.bfloat16)
        weigh(j, z)
        slot((j, 0))

    tile_n = min(256, rows)
    tiles_in = rows // tile_n
    tiles = spread * tiles_in

    def out_copy(i):
        at = pl.ds(i * tile_n, tile_n)
        return pltpu.make_async_copy(result.at[at], out.at[at], out_sem.at[i])

    def exchange(j, low, high):
        def body(i, carry):
            s, r = i // tiles_in, i % tiles_in
            at = pl.ds(pl.multiple_of(r * tile_n, tile_n), tile_n)
            lhs = jnp.concatenate([left[j, s, p, at, :] for p in range(aux)], axis=1)
            part = jnp.dot(lhs, wt[j], preferred_element_type=jnp.float32)
            to = pl.ds(pl.multiple_of(i * tile_n, tile_n), tile_n)
            if j > 0:
                part = total[to, :] + part
            if j == chunks - 1:
                result[to, :] = (part * scale).astype(jnp.bfloat16)
            else:
                total[to, :] = part
            return carry

        lax.fori_loop(low, high, body, 0)

    ran = []
    closed = [0] * chunks
    work = []

    def slot(event):
        if event is not None:
            line_event(*event)
        ran.append(event)
        n = len(ran) - 1
        for stage in range(3):
            if 0 <= n - 1 - stage and ran[n - 1 - stage] is not None:
                j, d = ran[n - 1 - stage]
                for p, there in members(d):
                    left_stage(j, p, there, stage)
        if n >= 4 and ran[n - 4] is not None:
            j, d = ran[n - 4]
            for p, there in members(d):
                left_close(j, p, there)
            closed[j] += 1
            if closed[j] == aux and j < chunks - 1:
                step = -(-tiles // max(1, aux - 1))
                work.extend((j, low, min(tiles, low + step)) for low in range(0, tiles, step))

    events = [(j, d) for j in range(chunks) for d in range(1, aux)]
    ring_own(0)
    if chunks > 1:
        ring_own(1)
    for i in range(load_groups // 2):
        mask_group(i)
    ring_step(0, 1)
    for i in range(load_groups // 2, load_groups):
        mask_group(i)
    for h in range(1, groups - 1):
        if h > 1:
            ring_step(0, h)
        half_dots(0, h - 1)
        if chunks > 1:
            ring_step(1, h)
            half_dots(1, h - 1)
    if groups > 2:
        ring_step(0, groups - 1)
    if chunks > 2:
        ring_own(2)
    half_dots(0, groups - 2)
    half_dots(0, groups - 1)
    close_half(0)
    if chunks > 1:
        ring_step(1, groups - 1)
        half_dots(1, groups - 2)
        half_dots(1, groups - 1)
        close_half(1)
    for j in range(2, chunks):
        for h in range(1, groups):
            ring_step(j, h)
            half_dots(j, h - 1)
            if h in (half_ring, groups - 1) and events and events[0][0] < j - 1:
                slot(events.pop(0))
        if j + 1 < chunks:
            ring_own(j + 1)
        half_dots(j, groups - 1)
        close_half(j)
    for event in events:
        slot(event)
        if work:
            exchange(*work.pop(0))
    for _ in range(4):
        if work:
            exchange(*work.pop(0))
        slot(None)
    for item in work:
        exchange(*item)
    parts = 4 if tiles % 4 == 0 else 1
    for i in range(parts):
        low, high = i * tiles // parts, (i + 1) * tiles // parts
        exchange(chunks - 1, low, high)
        if i > 0:
            for n in range((i - 1) * tiles // parts, low):
                out_copy(n).start()
    for n in range((parts - 1) * tiles // parts, tiles):
        out_copy(n).start()
    for action in finish:
        action()
    for n in range(tiles):
        out_copy(n).wait()


def shards(integrals, screen, coefficients, weights):
    _, rows, basis = integrals.shape
    occ = coefficients.shape[1]
    bas, aux = lax.axis_size("bas"), lax.axis_size("aux")
    groups, spread, chunks = bas // 2, bas // aux, occ // LANES
    sets = spread // 2
    tiles = spread * rows // min(256, rows)
    scale = 1.0 / math.sqrt(integrals.shape[0] * aux * occ)
    dma = pltpu.SemaphoreType.DMA
    bf16, f32 = jnp.bfloat16, jnp.float32
    return pl.pallas_call(
        functools.partial(kernel, groups, aux, scale),
        out_shape=jax.ShapeDtypeStruct((spread * rows, rows), bf16),
        in_specs=[
            pl.BlockSpec(memory_space=pl.ANY),
            pl.BlockSpec(memory_space=pltpu.SMEM),
            pl.BlockSpec(memory_space=pl.ANY),
            pl.BlockSpec(memory_space=pltpu.VMEM),
        ],
        out_specs=pl.BlockSpec(memory_space=pl.ANY),
        scratch_shapes=[
            pltpu.VMEM((rows, basis), bf16),
            pltpu.VMEM((chunks, bas, rows, LANES), bf16),
            pltpu.VMEM((chunks, rows, LANES), f32),
            pltpu.VMEM((chunks, aux, rows, LANES), bf16),
            pltpu.VMEM((chunks, spread, aux, rows, LANES), bf16),
            pltpu.VMEM((chunks, aux * LANES, rows), bf16),
            pltpu.VMEM((spread * rows, rows), f32),
            pltpu.VMEM((spread * rows, rows), bf16),
            dma((chunks + 8,)),
            dma((chunks, groups, 2)), dma((chunks, groups, 2)),
            dma((chunks, groups, 2)), dma((chunks, groups, 2)),
            dma((chunks, aux)), dma((chunks, aux)), dma((chunks, aux)),
            dma((chunks, sets, aux, 2)), dma((chunks, sets, aux, 2)),
            dma((chunks, sets, aux, 2)), dma((chunks, sets, aux, 2)),
            dma((chunks, sets, aux)),
            dma((tiles,)),
        ],
        compiler_params=pltpu.CompilerParams(
            collective_id=0, has_side_effects=True, vmem_limit_bytes=62 * 1024 * 1024),
    )(integrals, screen, coefficients, weights.reshape(1, occ))


def solution(mesh):
    in_specs = (P("aux", "bas", None), P("aux", "bas", None), P("bas", None), P())
    out_specs = P("aux", "bas")
    return jax.shard_map(shards, mesh=mesh, in_specs=in_specs, out_specs=out_specs, check_vma=False)
```

```python
import functools
import math

import jax
import jax.numpy as jnp
from jax import lax
from jax.experimental import pallas as pl
from jax.experimental.pallas import tpu as pltpu
from jax.sharding import PartitionSpec as P

BLOCK = 128
LANES = 128


def kernel(groups, aux, scale, integrals, screen, coefs, weights, out,
           ints, fac, acc, right, left, wt, total, result,
           load_sem, ring_send, ring_recv, pair_send, pair_recv,
           line_recv, up_send, down_send,
           lring_send, lring_recv, lpair_send, lpair_recv, lown_sem, out_sem):
    rows, basis = ints.shape
    chunks = fac.shape[0]
    half_rows = rows // 2
    spread = left.shape[1]
    sets = spread // 2
    row_blocks = rows // BLOCK
    col_blocks = basis // BLOCK
    bas_me = lax.axis_index("bas")
    z = lax.axis_index("aux")
    core = bas_me % 2
    half_ring = groups // 2

    def swap(index):
        upper = index // half_ring
        return index + upper * (3 * half_ring - 1 - 2 * index)

    pos = swap(bas_me // 2)

    def device_at(position, which):
        return 2 * swap(position % groups) + which

    partner = bas_me - core + (1 - core)

    def ring_to(half):
        return device_at(pos + groups + 1 - 2 * half, core)

    def remote(src, dst, send, recv, bas=None, aux_to=None):
        return pltpu.make_async_remote_copy(
            src_ref=src, dst_ref=dst, send_sem=send, recv_sem=recv,
            device_id={"bas": bas_me if bas is None else bas, "aux": z if aux_to is None else aux_to},
            device_id_type=pl.DeviceIdType.MESH)

    finish = []

    load_groups = 8
    load_cols = basis // load_groups

    def int_load(i):
        cols = pl.ds(i * load_cols, load_cols)
        return pltpu.make_async_copy(integrals.at[0, :, cols], ints.at[:, cols], load_sem.at[chunks + i])

    def fac_load(j):
        return pltpu.make_async_copy(coefs.at[:, pl.ds(j * LANES, LANES)], fac.at[j, bas_me], load_sem.at[j])

    for j in range(chunks):
        fac_load(j).start()
    for i in range(load_groups):
        int_load(i).start()

    barrier = pltpu.get_barrier_semaphore()
    for other in (ring_to(0), ring_to(1), partner):
        pl.semaphore_signal(barrier, inc=1, device_id={"bas": other, "aux": z}, device_id_type=pl.DeviceIdType.MESH)

    @pl.when(z > 0)
    def _():
        pl.semaphore_signal(barrier, inc=1, device_id={"bas": bas_me, "aux": z - 1}, device_id_type=pl.DeviceIdType.MESH)

    @pl.when(z < aux - 1)
    def _():
        pl.semaphore_signal(barrier, inc=1, device_id={"bas": bas_me, "aux": z + 1}, device_id_type=pl.DeviceIdType.MESH)

    peers = 3 + (z + aux - 1) // aux + (2 * aux - 2 - z) // aux
    pl.semaphore_wait(barrier, peers)

    def origin(h, half, which):
        return device_at(pos + groups - h + 2 * h * half, which)

    def fac_piece(j, h, half, which):
        return fac.at[j, origin(h, half, which), pl.ds(half * half_rows, half_rows)]

    def ring_copy(j, h, half):
        piece = fac_piece(j, h, half, core)
        return remote(piece, piece, ring_send.at[j, h, half], ring_recv.at[j, h, half], bas=ring_to(half))

    def pair_copy(j, h, half):
        piece = fac_piece(j, h, half, core)
        return remote(piece, piece, pair_send.at[j, h, half], pair_recv.at[j, h, half], bas=partner)

    def pass_on(j, h, half):
        if h < groups - 1:
            ring_copy(j, h, half).start()
            finish.append(ring_copy(j, h, half).wait_send)
        pair_copy(j, h, half).start()
        finish.append(pair_copy(j, h, half).wait_send)

    def ring_own(j):
        fac_load(j).wait()
        for half in (0, 1):
            pass_on(j, 0, half)

    def ring_step(j, h):
        for half in (0, 1):
            piece = fac_piece(j, h, half, core)
            remote(piece, piece, ring_send.at[j, h - 1, half], ring_recv.at[j, h - 1, half], bas=ring_to(half)).wait_recv()
            pass_on(j, h, half)

    def pair_wait(j, h):
        for half in (0, 1):
            piece = fac_piece(j, h, half, 1 - core)
            remote(piece, piece, pair_send.at[j, h, half], pair_recv.at[j, h, half], bas=partner).wait_recv()

    def mask_group(i):
        int_load(i).wait()
        per = col_blocks // load_groups

        def body(q, carry):
            column = i * per + q
            cols = pl.ds(pl.multiple_of(column * BLOCK, BLOCK), BLOCK)
            for r in range(row_blocks):
                keep = screen[0, r, column].astype(jnp.float32)
                keep = jnp.full((BLOCK, BLOCK), keep, jnp.float32).astype(jnp.bfloat16)
                ints[pl.ds(r * BLOCK, BLOCK), cols] = ints[pl.ds(r * BLOCK, BLOCK), cols] * keep
            return carry

        lax.fori_loop(0, per, body, 0)

    tile_m = min(256, rows)
    fine = half_rows % LANES == 0

    def piece_dot(j, block, start, length, first):
        def body(m, carry):
            at = pl.ds(pl.multiple_of(m * tile_m, tile_m), tile_m)
            cols = pl.ds(pl.multiple_of(block * rows + start, LANES), length)
            part = jnp.dot(ints[at, cols], fac[j, block, pl.ds(start, length), :],
                           preferred_element_type=jnp.float32)
            acc[j, at, :] = part if first else acc[j, at, :] + part
            return carry

        lax.fori_loop(0, rows // tile_m, body, 0)

    def half_dots(j, h):
        pair_wait(j, h)
        if fine:
            if h == 0:
                piece_dot(j, bas_me, 0, rows, True)
                piece_dot(j, partner, 0, rows, False)
            else:
                for half in (0, 1):
                    for which in (core, 1 - core):
                        piece_dot(j, origin(h, half, which), half * half_rows, half_rows, False)
        elif h == groups - 1:
            acc[j] = jnp.zeros(acc.shape[1:], acc.dtype)

            def body(block, carry):
                piece_dot(j, block, 0, rows, False)
                return carry

            lax.fori_loop(0, 2 * groups, body, 0)

    def weigh(j, p):
        values = right[j, p].astype(jnp.float32) * weights[:, pl.ds(j * LANES, LANES)]
        wt[j, pl.ds(pl.multiple_of(p * LANES, LANES), LANES), :] = values.T.astype(jnp.bfloat16)

    def up_copy(j, p):
        return remote(right.at[j, p], right.at[j, p], up_send.at[j, p], line_recv.at[j, p], aux_to=z + 1)

    def down_copy(j, p):
        return remote(right.at[j, p], right.at[j, p], down_send.at[j, p], line_recv.at[j, p], aux_to=z - 1)

    def guard(condition, action):
        pl.when(condition)(lambda: action())

    def send_up(j, p, condition):
        condition = condition & (z < aux - 1)
        guard(condition, lambda: up_copy(j, p).start())
        finish.append(lambda: guard(condition, lambda: up_copy(j, p).wait_send()))

    def send_down(j, p, condition):
        condition = condition & (z > 0)
        guard(condition, lambda: down_copy(j, p).start())
        finish.append(lambda: guard(condition, lambda: down_copy(j, p).wait_send()))

    def left_piece(ref_index, half):
        j, s, p = ref_index
        return left.at[j, s, p, pl.ds(half * half_rows, half_rows)]

    def lring_copy(src, j, t, p, half):
        return remote(src, left_piece((j, 2 * t + core, p), half),
                      lring_send.at[j, t, p, half], lring_recv.at[j, t, p, half], bas=ring_to(half))

    def lpair_copy(src, j, t, p, half):
        return remote(src, left_piece((j, 2 * t + core, p), half),
                      lpair_send.at[j, t, p, half], lpair_recv.at[j, t, p, half], bas=partner)

    def lown_copy(j, t, p):
        return pltpu.make_async_copy(right.at[j, p], left.at[j, 2 * t + core, p], lown_sem.at[j, t, p])

    def away(t):
        return (pos - swap(z * sets + t) + groups) % groups

    def left_start(j, p, condition):
        for t in range(sets):
            mine = condition & (away(t) == 0)

            def go(t=t):
                for half in (0, 1):
                    src = right.at[j, p, pl.ds(half * half_rows, half_rows)]
                    lring_copy(src, j, t, p, half).start()
                    lpair_copy(src, j, t, p, half).start()
                lown_copy(j, t, p).start()

            def end(t=t):
                for half in (0, 1):
                    src = right.at[j, p, pl.ds(half * half_rows, half_rows)]
                    lring_copy(src, j, t, p, half).wait_send()
                    lpair_copy(src, j, t, p, half).wait_send()

            guard(mine, go)
            finish.append(lambda mine=mine, end=end: guard(mine, end))

    def left_stage(j, p, condition, stage):
        for t in range(sets):
            distance = away(t)
            side = (2 * distance) // (groups + 1)
            middle = distance == half_ring
            other = condition & (distance != 0)
            takes = other & (middle if stage == 1 else distance != half_ring)
            halves = (0, 1) if stage == 1 else (side if stage == 0 else 1 - side,)
            for half in halves:
                hops = distance + half * (groups - 2 * distance)
                src = left_piece((j, 2 * t + core, p), half)

                def go(t=t, half=half, src=src):
                    lring_copy(src, j, t, p, half).wait_recv()
                    lpair_copy(src, j, t, p, half).start()

                def onward(t=t, half=half, src=src):
                    lring_copy(src, j, t, p, half).start()

                def end(t=t, half=half, src=src):
                    lpair_copy(src, j, t, p, half).wait_send()

                def end_onward(t=t, half=half, src=src):
                    lring_copy(src, j, t, p, half).wait_send()

                further = takes & (hops < groups - 1)
                guard(takes, go)
                guard(further, onward)
                finish.append(lambda takes=takes, end=end: guard(takes, end))
                finish.append(lambda further=further, end=end_onward: guard(further, end))

    def left_close(j, p, condition):
        for t in range(sets):
            mine = condition & (away(t) == 0)

            def own(t=t):
                lown_copy(j, t, p).wait()

            guard(mine, own)

            def from_partner(t=t):
                for half in (0, 1):
                    dst = left_piece((j, 2 * t + 1 - core, p), half)
                    remote(dst, dst, lpair_send.at[j, t, p, half], lpair_recv.at[j, t, p, half], bas=partner).wait_recv()

            guard(condition, from_partner)

    always = z >= 0

    def members(d):
        if d == 0:
            return [(z, always)]
        return [(z - d, z - d >= 0), (z + d, z + d < aux)]

    def line_event(j, d):
        for n, (p, there) in enumerate(members(d)):
            if d > 0:
                guard(there, lambda p=p: up_copy(j, p).wait_recv())
            if d == 0 or n == 0:
                send_up(j, p, there)
            if d == 0 or n == 1:
                send_down(j, p, there)
            left_start(j, p, there)
        if d > 0:
            for p, there in members(d):
                guard(there, lambda p=p: weigh(j, p))

    def close_half(j):
        right[j, z] = acc[j].astype(jnp.bfloat16)
        weigh(j, z)
        slot((j, 0))

    tile_n = min(256, rows)
    tiles_in = rows // tile_n
    tiles = spread * tiles_in

    def out_copy(i):
        at = pl.ds(i * tile_n, tile_n)
        return pltpu.make_async_copy(result.at[at], out.at[at], out_sem.at[i])

    def exchange(j, low, high):
        def body(i, carry):
            s, r = i // tiles_in, i % tiles_in
            at = pl.ds(pl.multiple_of(r * tile_n, tile_n), tile_n)
            lhs = jnp.concatenate([left[j, s, p, at, :] for p in range(aux)], axis=1)
            part = jnp.dot(lhs, wt[j], preferred_element_type=jnp.float32)
            to = pl.ds(pl.multiple_of(i * tile_n, tile_n), tile_n)
            if j > 0:
                part = total[to, :] + part
            if j == chunks - 1:
                result[to, :] = (part * scale).astype(jnp.bfloat16)
            else:
                total[to, :] = part
            return carry

        lax.fori_loop(low, high, body, 0)

    ran = []
    closed = [0] * chunks
    work = []

    def slot(event):
        if event is not None:
            line_event(*event)
        ran.append(event)
        n = len(ran) - 1
        for stage in range(3):
            if 0 <= n - 1 - stage and ran[n - 1 - stage] is not None:
                j, d = ran[n - 1 - stage]
                for p, there in members(d):
                    left_stage(j, p, there, stage)
        if n >= 4 and ran[n - 4] is not None:
            j, d = ran[n - 4]
            for p, there in members(d):
                left_close(j, p, there)
            closed[j] += 1
            if closed[j] == aux and j < chunks - 1:
                step = -(-tiles // max(1, aux - 1))
                work.extend((j, low, min(tiles, low + step)) for low in range(0, tiles, step))

    events = [(j, d) for j in range(chunks) for d in range(1, aux)]
    ring_own(0)
    if chunks > 1:
        ring_own(1)
    for i in range(load_groups // 2):
        mask_group(i)
    ring_step(0, 1)
    for i in range(load_groups // 2, load_groups):
        mask_group(i)
    for h in range(1, groups - 1):
        if h > 1:
            ring_step(0, h)
        half_dots(0, h - 1)
        if chunks > 1:
            ring_step(1, h)
            half_dots(1, h - 1)
    if groups > 2:
        ring_step(0, groups - 1)
    if chunks > 2:
        ring_own(2)
    half_dots(0, groups - 2)
    half_dots(0, groups - 1)
    close_half(0)
    if chunks > 1:
        ring_step(1, groups - 1)
        half_dots(1, groups - 2)
        half_dots(1, groups - 1)
        close_half(1)
    for j in range(2, chunks):
        for h in range(1, groups):
            ring_step(j, h)
            half_dots(j, h - 1)
            if h in (half_ring, groups - 1) and events and events[0][0] < j - 1:
                slot(events.pop(0))
        if j + 1 < chunks:
            ring_own(j + 1)
        half_dots(j, groups - 1)
        close_half(j)
    for event in events:
        slot(event)
        if work:
            exchange(*work.pop(0))
    for _ in range(4):
        if work:
            exchange(*work.pop(0))
        slot(None)
    for item in work:
        exchange(*item)
    parts = 4 if tiles % 4 == 0 else 1
    for i in range(parts):
        low, high = i * tiles // parts, (i + 1) * tiles // parts
        exchange(chunks - 1, low, high)
        if i > 0:
            for n in range((i - 1) * tiles // parts, low):
                out_copy(n).start()
    for n in range((parts - 1) * tiles // parts, tiles):
        out_copy(n).start()
    for action in finish:
        action()
    for n in range(tiles):
        out_copy(n).wait()


def shards(integrals, screen, coefficients, weights):
    _, rows, basis = integrals.shape
    occ = coefficients.shape[1]
    bas, aux = lax.axis_size("bas"), lax.axis_size("aux")
    groups, spread, chunks = bas // 2, bas // aux, occ // LANES
    sets = spread // 2
    tiles = spread * rows // min(256, rows)
    scale = 1.0 / math.sqrt(integrals.shape[0] * aux * occ)
    dma = pltpu.SemaphoreType.DMA
    bf16, f32 = jnp.bfloat16, jnp.float32
    return pl.pallas_call(
        functools.partial(kernel, groups, aux, scale),
        out_shape=jax.ShapeDtypeStruct((spread * rows, rows), bf16),
        in_specs=[
            pl.BlockSpec(memory_space=pl.ANY),
            pl.BlockSpec(memory_space=pltpu.SMEM),
            pl.BlockSpec(memory_space=pl.ANY),
            pl.BlockSpec(memory_space=pltpu.VMEM),
        ],
        out_specs=pl.BlockSpec(memory_space=pl.ANY),
        scratch_shapes=[
            pltpu.VMEM((rows, basis), bf16),
            pltpu.VMEM((chunks, bas, rows, LANES), bf16),
            pltpu.VMEM((chunks, rows, LANES), f32),
            pltpu.VMEM((chunks, aux, rows, LANES), bf16),
            pltpu.VMEM((chunks, spread, aux, rows, LANES), bf16),
            pltpu.VMEM((chunks, aux * LANES, rows), bf16),
            pltpu.VMEM((spread * rows, rows), f32),
            pltpu.VMEM((spread * rows, rows), bf16),
            dma((chunks + 8,)),
            dma((chunks, groups, 2)), dma((chunks, groups, 2)),
            dma((chunks, groups, 2)), dma((chunks, groups, 2)),
            dma((chunks, aux)), dma((chunks, aux)), dma((chunks, aux)),
            dma((chunks, sets, aux, 2)), dma((chunks, sets, aux, 2)),
            dma((chunks, sets, aux, 2)), dma((chunks, sets, aux, 2)),
            dma((chunks, sets, aux)),
            dma((tiles,)),
        ],
        compiler_params=pltpu.CompilerParams(
            collective_id=0, has_side_effects=True, vmem_limit_bytes=62 * 1024 * 1024),
    )(integrals, screen, coefficients, weights.reshape(1, occ))


def solution(mesh):
    in_specs = (P("aux", "bas", None), P("aux", "bas", None), P("bas", None), P())
    out_specs = P("aux", "bas")
    return jax.shard_map(shards, mesh=mesh, in_specs=in_specs, out_specs=out_specs, check_vma=False)
```
